256 devices in a mesh: row: 32 (over y, z_hi, x), col: 8 (over z_lo, core).
Axes of the slice: x: 4, y: 4, z: 8 (z_hi: 2, z_lo: 4; z = z_hi * 4 + z_lo), core: 2. Of those that a mesh axis runs over, the one named last changes fastest.
Arguments:
- tokens: bfloat16 [2048, 8192], P('row', 'col'), may hold values from -6 to 6
- gate_up: bfloat16 [8192, 2, 16384], P('col', None, 'row'), may hold values from -0.0625 to 0.0625
- cotangent: bfloat16 [2048, 16384], P('col', 'row'), may hold values from -6 to 6
Outputs:
- hidden: bfloat16 [2048, 16384], P('col', 'row')
- input_grad: bfloat16 [2048, 8192], P('row', 'col')
- weight_grad: bfloat16 [8192, 2, 16384], P('col', None, 'row')
The draws below stay inside these ranges and needn't reach their ends.
All inputs are finite; a program needn't handle non-finite values.
Results may differ from the reference program's by a relative error of at most 0.0049.
Values may be sent and summed in bfloat16 or wider, within the bound.
No kernel may reach another device: no remote copies, remote signals or barrier semaphores. Data moves between devices by JAX's collectives and lax.ppermute only.
A program may use at most 128 MiB of HBM per device.

```python
import jax
import jax.numpy as jnp
from jax import lax

D = 8192
FF = 16384
TOKENS = 2048


def raised(result, stream_key, source, target, blocks, factor):
    def block_of(dim):
        return (jnp.arange(result.shape[dim]) // (result.shape[dim] // blocks)).reshape((-1,) + (1,) * (result.ndim - 1 - dim))

    first = jax.random.permutation(stream_key, blocks)[block_of(target)]
    far = (block_of(target) + blocks // 2) % blocks
    return jnp.where((block_of(source) == first) | (block_of(source) == far), factor * result, result)


def block_levels(stream_key, shape, cuts, low, top_value):
    gain, own = 1.0, jax.random.fold_in(stream_key, 6)
    for axis_at, blocks in cuts:
        steps = jnp.exp(jax.random.uniform(jax.random.fold_in(own, axis_at), (blocks,), jnp.float32, low / len(cuts), top_value / len(cuts)))
        gain = gain * jnp.repeat(steps, shape[axis_at] // blocks).reshape([-1 if axis == axis_at else 1 for axis in range(len(shape))])
    return gain


def scatter_about(rng, extent, scale, limit, shards=(), held_as=jnp.bfloat16):
    values = jax.random.normal(rng, extent, jnp.float32) * scale
    if len(shards) > 0:
        values = block_levels(rng, extent, shards, -0.22, 0.18) * values
    return jnp.clip(values, min=-limit, max=limit).astype(held_as)


def heavy_noise(stream_key, shape, spread, reach, cuts, heavy, held_as=jnp.bfloat16):
    values = spread * jax.random.normal(stream_key, shape, jnp.float32)
    if cuts:
        values = values * block_levels(stream_key, shape, cuts, -0.22, 0.18)
    return jnp.clip(raised(values, jax.random.fold_in(stream_key, 3), *heavy), -reach, reach).astype(held_as)


def setup_inputs(seed: int = 0) -> dict:
    splits = jax.random.split(jax.random.key(seed), 4)
    tokens = scatter_about(splits[0], (TOKENS, D), 1.0, 6.0, ((0, 32), (1, 8)))
    gate_up = scatter_about(splits[1], (D, 2, FF), D ** -0.5, 0.0625, ((0, 8), (2, 32)))
    cotangent = heavy_noise(splits[2], (TOKENS, FF), 1.0, 6.0, ((0, 8), (1, 32)), (1, 0, 32, 2.75))
    return {"tokens": tokens, "gate_up": gate_up, "cotangent": cotangent}


def reference(tokens, gate_up, cotangent):
    weights = gate_up.reshape(D, 2 * FF)
    combined = jnp.dot(tokens, weights, preferred_element_type=jnp.float32)
    gate_pre = combined[:, :FF]
    up_pre = combined[:, FF:]
    sigmoid = jax.nn.sigmoid(gate_pre)
    activated = gate_pre * sigmoid
    hidden = (activated * up_pre).astype(jnp.bfloat16)
    grad_out = cotangent.astype(jnp.float32)
    grad_gate = grad_out * up_pre * sigmoid * (1.0 + gate_pre * (1.0 - sigmoid))
    grad_up = grad_out * activated
    stacked = jnp.stack([grad_gate, grad_up], axis=1).astype(jnp.bfloat16)
    flat_grads = stacked.reshape(TOKENS, 2 * FF)
    weight_grad = lax.dot_general(tokens, flat_grads, (((0,), (0,)), ((), ())),
                                  preferred_element_type=jnp.float32)
    weight_grad = weight_grad.astype(jnp.bfloat16).reshape(D, 2, FF)
    input_grad = lax.dot_general(flat_grads, weights, (((1,), (1,)), ((), ())),
                                 preferred_element_type=jnp.float32)
    return hidden, input_grad.astype(jnp.bfloat16), weight_grad
```

```python
import jax
import jax.numpy as jnp
from jax import lax
from jax.sharding import Mesh
from jax.sharding import PartitionSpec as P

AXES = ("y", "zh", "x", "zl", "c")
CHUNKS = 1
BF16 = jnp.bfloat16
F32 = jnp.float32


def xor_perm(n, k):
    return [(i, i ^ k) for i in range(n)]


def plane_perm(k, x_core):
    pairs = []
    for y in range(4):
        for x in range(4):
            for c in range(2):
                y2, x2 = (y, x ^ k) if c == x_core else (y ^ k, x)
                pairs.append(((y * 4 + x) * 2 + c, (y2 * 4 + x2) * 2 + c))
    return pairs


def send_plane(value, k, x_core):
    return lax.ppermute(value, ("y", "x", "c"), plane_perm(k, x_core))


def pick(value, index):
    return lax.dynamic_index_in_dim(value, index, 0, keepdims=False)


def xor_rows(value, index):
    return jnp.stack([pick(value, index ^ k) for k in range(4)])


def on_device(tokens, gate_up, cotangent):
    rows, feats = tokens.shape
    half = gate_up.shape[2]
    y, zh, x, zl, c = (lax.axis_index(a) for a in AXES)
    shift = y ^ zl
    same = zh == c
    core0 = c == 0
    fwd_a, fwd_b = [(0, 2), (3, 1), (1, 0), (2, 3)], [(1, 2), (2, 1)]
    back_a = [(b, a) for a, b in fwd_a]

    recv_a = lax.ppermute(tokens, ("zh", "c"), fwd_a)
    recv_b = lax.ppermute(tokens, ("zh", "c"), fwd_b)
    own = jnp.where(same, tokens, recv_a)
    sib = jnp.where(same, recv_a, recv_b)
    block = jnp.concatenate([own, sib], axis=1)

    w_own = gate_up.reshape(feats, 2 * half)
    w_sib = lax.ppermute(w_own, "c", xor_perm(2, 1))
    weights = jnp.concatenate([w_own, w_sib], axis=0)

    line = jnp.stack([block] + [send_plane(block, k, 0) for k in (1, 2, 3)])
    size = rows // CHUNKS
    cot = xor_rows(cotangent.reshape(4, rows, half), x)

    hiddens, in_grads, toks, gs = [], [], [], []
    for j in range(CHUNKS):
        part = lax.slice_in_dim(line, j * size, (j + 1) * size, axis=1)
        plane = jnp.stack([part] + [send_plane(part, k, 1) for k in (1, 2, 3)])
        flat = plane.reshape(16 * size, 2 * feats)
        pre = jnp.dot(flat, weights, preferred_element_type=F32)
        pre = pre.reshape(4, 4, size, 2 * half)

        def slab(k):
            major = lax.dynamic_index_in_dim(pre, shift ^ k, 0, keepdims=False)
            minor = lax.dynamic_index_in_dim(pre, shift ^ k, 1, keepdims=False)
            return jnp.where(core0, major, minor)

        total = slab(0)
        for k in (1, 2, 3):
            total = total + lax.ppermute(
                slab(k).astype(BF16), "zl", xor_perm(4, k)
            ).astype(F32)
        gate_pre, up_pre = total[..., :half], total[..., half:]
        sigmoid = jax.nn.sigmoid(gate_pre)
        activated = gate_pre * sigmoid
        hiddens.append((activated * up_pre).astype(BF16))
        grad_out = lax.slice_in_dim(cot, j * size, (j + 1) * size, axis=1).astype(F32)
        grad_gate = grad_out * up_pre * sigmoid * (1.0 + gate_pre * (1.0 - sigmoid))
        grad_up = grad_out * activated
        grads = jnp.concatenate([grad_gate, grad_up], axis=-1).astype(BF16)

        gathered = jnp.stack(
            [grads] + [lax.ppermute(grads, "zl", xor_perm(4, k)) for k in (1, 2, 3)]
        )
        ordered = xor_rows(gathered, shift)
        ordered = jnp.where(core0, ordered, jnp.swapaxes(ordered, 0, 1))
        g_flat = ordered.reshape(16 * size, 2 * half)
        out = lax.dot_general(
            g_flat, weights, (((1,), (1,)), ((), ())), preferred_element_type=F32
        ).reshape(4, 4, size, 2 * feats)
        for send in (1, 0):
            part = out[0]
            for k in (1, 2, 3):
                part = part + send_plane(out[k].astype(BF16), k, send).astype(F32)
            out = part
        g_own, g_sib = out[:, :feats].astype(BF16), out[:, feats:].astype(BF16)
        recv_a = lax.ppermute(jnp.where(same, g_sib, g_own), ("zh", "c"), back_a)
        recv_b = lax.ppermute(g_sib, ("zh", "c"), fwd_b)
        first = jnp.where(same, out[:, :feats], recv_b.astype(F32))
        in_grads.append((first + recv_a.astype(F32)).astype(BF16))
        toks.append(flat)
        gs.append(g_flat)

    t_all, g_all = jnp.concatenate(toks, axis=0), jnp.concatenate(gs, axis=0)
    t_sib = lax.ppermute(t_all[:, feats:], "c", xor_perm(2, 1))
    g_sib = lax.ppermute(g_all, "c", xor_perm(2, 1))

    def outer(t, g):
        return lax.dot_general(t, g, (((0,), (0,)), ((), ())), preferred_element_type=F32)

    weight_grad = outer(t_all[:, :feats], g_all) + outer(t_sib, g_sib)
    weight_grad = weight_grad.astype(BF16).reshape(feats, 2, half)
    hidden = xor_rows(jnp.concatenate(hiddens, axis=1), x).reshape(4 * rows, half)
    return hidden, jnp.concatenate(in_grads, axis=0), weight_grad


def solution(mesh):
    split = Mesh(mesh.devices.reshape(4, 2, 4, 4, 2), AXES)
    row, col = ("y", "zh", "x"), ("zl", "c")
    in_specs = (P(row, col), P(col, None, row), P(col, row))
    out_specs = (P(col, row), P(row, col), P(col, None, row))
    return jax.shard_map(
        on_device, mesh=split, in_specs=in_specs, out_specs=out_specs, check_vma=False
    )
```

```python
import itertools

import jax
import jax.numpy as jnp
from jax import lax
from jax.sharding import Mesh
from jax.sharding import PartitionSpec as P

SIZES = {"y": 4, "zh": 2, "x": 4, "zl": 4, "c": 2}
BF16 = jnp.bfloat16
F32 = jnp.float32


def permute(value, axes, target):
    def flat(place):
        index = 0
        for a in axes:
            index = index * SIZES[a] + place[a]
        return index

    pairs = []
    for coords in itertools.product(*(range(SIZES[a]) for a in axes)):
        place = dict(zip(axes, coords))
        moved = target(place)
        if moved is not None:
            pairs.append((flat(place), flat({**place, **moved})))
    return lax.ppermute(value, axes, pairs)


def plane(value, k, x_core):
    def target(p):
        return {"x": p["x"] ^ k} if p["c"] == x_core else {"y": p["y"] ^ k}

    return permute(value, ("y", "x", "c"), target)


def line(value, k):
    return permute(value, ("zl",), lambda p: {"zl": p["zl"] ^ k})


def swap(value):
    return permute(value, ("c",), lambda p: {"c": 1 - p["c"]})


def spread_a(p):
    return {"zh": 1 - p["zh"]} if p["zh"] == p["c"] else {"c": p["zh"]}


def spread_b(p):
    return None if p["zh"] == p["c"] else {"zh": 1 - p["zh"], "c": p["zh"]}


def spread_far_a(p):
    return {**spread_a(p), "zl": p["zl"] ^ 1}


def spread_far_b(p):
    return {**(spread_b(p) or {}), "zl": p["zl"] ^ 1}


def collect_a(p):
    return {"c": 1 - p["c"]} if p["zh"] == p["c"] else {"zh": 1 - p["zh"]}


def collect_far_a(p):
    return {**collect_a(p), "zl": p["zl"] ^ 1}


def pick(value, index, axis=0):
    return lax.dynamic_index_in_dim(value, index, axis, keepdims=False)


def xor_rows(value, index):
    return jnp.stack([pick(value, index ^ k) for k in range(4)])


def outer(t, g):
    return lax.dot_general(t, g, (((0,), (0,)), ((), ())), preferred_element_type=F32)


def on_device(tokens, gate_up, cotangent):
    rows, feats = tokens.shape
    half = gate_up.shape[2]
    part = rows // 2
    y, zh, x, zl, c = (lax.axis_index(a) for a in ("y", "zh", "x", "zl", "c"))
    shift = y ^ zl
    bit = zl & 1
    same = zh == c
    core0 = c == 0
    near_axes, far_axes = ("zh", "c"), ("zh", "zl", "c")

    halves = tokens.reshape(2, part, feats)
    mine, other = pick(halves, bit), pick(halves, 1 - bit)
    recv_a = permute(tokens, near_axes, spread_a)
    recv_b = permute(tokens, near_axes, spread_b)
    far_a = permute(other, far_axes, spread_far_a)
    far_b = permute(other, far_axes, spread_far_b)
    recv_a = recv_a.reshape(2, part, feats)
    recv_b = recv_b.reshape(2, part, feats)

    def two(local, index):
        a, b = pick(recv_a, index), pick(recv_b, index)
        return [jnp.where(same, local, a), jnp.where(same, a, b)]

    far = [jnp.where(same, far_b, far_a), jnp.where(same, far_a, far_b)]
    block = jnp.concatenate(two(mine, bit) + far, axis=1)
    extra = jnp.concatenate(two(other, 1 - bit), axis=1)

    w_own = gate_up.reshape(feats, 2 * half)
    w_far = line(w_own, 1)
    w_near = jnp.concatenate([w_own, swap(w_own)], axis=0)
    w_far = jnp.concatenate([w_far, swap(w_far)], axis=0)

    lines = jnp.stack([block] + [plane(block, k, 0) for k in (1, 2, 3)])
    planes = [lines] + [plane(lines, k, 1) for k in (1, 2, 3)]
    *planes, extra = lax.optimization_barrier(tuple(planes) + (extra,))
    extra = lax.all_gather(extra, ("y", "x"), axis=0, tiled=True)
    toks = jnp.stack(planes).reshape(16 * part, 4 * feats)
    pre = jnp.dot(toks[:, : 2 * feats], w_near, preferred_element_type=F32)
    pre = pre + jnp.dot(toks[:, 2 * feats :], w_far, preferred_element_type=F32)
    pre = pre.reshape(4, 4, part, 2 * half)

    def slab(k):
        major, minor = pick(pre, shift ^ k, 0), pick(pre, shift ^ k, 1)
        return jnp.where(core0, major, minor)

    recv = [line(slab(k).astype(BF16), k).astype(F32) for k in (1, 2, 3)]
    total = jnp.stack([slab(0) + recv[1], recv[0] + recv[2]])
    gate_pre, up_pre = total[..., :half], total[..., half:]
    sigmoid = jax.nn.sigmoid(gate_pre)
    activated = gate_pre * sigmoid
    hidden = (activated * up_pre).astype(BF16)
    cot = xor_rows(cotangent.reshape(4, 2, part, half), x)
    grad_out = jnp.stack([pick(cot, bit, 1), pick(cot, 1 - bit, 1)]).astype(F32)
    grad_gate = grad_out * up_pre * sigmoid * (1.0 + gate_pre * (1.0 - sigmoid))
    grad_up = grad_out * activated
    grads = jnp.concatenate([grad_gate, grad_up], axis=-1).astype(BF16)

    gathered = jnp.stack([grads[0]] + [line(grads[k & 1], k) for k in (1, 2, 3)])
    ordered = xor_rows(gathered, shift)
    ordered = jnp.where(core0, ordered, jnp.swapaxes(ordered, 0, 1))
    g_near = ordered.reshape(16 * part, 2 * half)
    weights = jnp.concatenate([w_near, w_far], axis=0)
    out = lax.dot_general(
        g_near, weights, (((1,), (1,)), ((), ())), preferred_element_type=F32
    ).reshape(4, 4, part, 4 * feats)

    g_far = xor_rows(line(gathered, 1), zl ^ 1)
    g_far = jnp.stack([pick(g_far, x ^ k, 1) for k in range(4)], axis=1)
    g_far = g_far.reshape(16 * part, 2 * half)
    weight_grad = outer(toks[:, :feats], g_near)
    weight_grad = weight_grad + outer(swap(toks[:, feats : 2 * feats]), swap(g_near))
    weight_grad = weight_grad + outer(extra[:, :feats], g_far)
    weight_grad = weight_grad + outer(swap(extra[:, feats:]), swap(g_far))
    weight_grad = weight_grad.astype(BF16).reshape(feats, 2, half)

    for send in (1, 0):
        first = out[0]
        recv = [plane(out[k].astype(BF16), k, send) for k in (1, 2, 3)]
        if send == 0:
            *recv, weight_grad = lax.optimization_barrier(tuple(recv) + (weight_grad,))
        for r in recv:
            first = first + r.astype(F32)
        out = first
    parts = [out[:, i * feats : (i + 1) * feats] for i in range(4)]
    low = [p.astype(BF16) for p in parts]
    recv_a = permute(jnp.where(same, low[1], low[0]), near_axes, collect_a)
    recv_b = permute(low[1], near_axes, spread_b)
    far_a = permute(jnp.where(same, low[3], low[2]), far_axes, collect_far_a)
    far_b = permute(jnp.where(same, low[2], low[3]), far_axes, spread_far_b)
    near = jnp.where(same, parts[0], recv_b.astype(F32)) + recv_a.astype(F32)
    far = far_a.astype(F32) + far_b.astype(F32)
    near, far = near.astype(BF16), far.astype(BF16)

    def join(a, b, axis):
        return jnp.where(bit == 0, jnp.stack([a, b], axis), jnp.stack([b, a], axis))

    input_grad = join(near, far, 0).reshape(rows, feats)
    hidden = xor_rows(join(hidden[0], hidden[1], 1), x).reshape(4 * rows, half)
    return hidden, input_grad, weight_grad


def solution(mesh):
    split = Mesh(mesh.devices.reshape(tuple(SIZES.values())), tuple(SIZES))
    row, col = ("y", "zh", "x"), ("zl", "c")
    in_specs = (P(row, col), P(col, None, row), P(col, row))
    out_specs = (P(col, row), P(row, col), P(col, None, row))
    return jax.shard_map(
        on_device, mesh=split, in_specs=in_specs, out_specs=out_specs, check_vma=False
    )
```

```python
import jax
import jax.numpy as jnp
from jax import lax
from jax.sharding import Mesh
from jax.sharding import PartitionSpec as P

AXES = ("y", "zh", "x", "zl", "c")
CHUNKS = 1
BF16 = jnp.bfloat16
F32 = jnp.float32


def xor_perm(n, k):
    return [(i, i ^ k) for i in range(n)]


def plane_perm(k, x_core):
    pairs = []
    for y in range(4):
        for x in range(4):
            for c in range(2):
                y2, x2 = (y, x ^ k) if c == x_core else (y ^ k, x)
                pairs.append(((y * 4 + x) * 2 + c, (y2 * 4 + x2) * 2 + c))
    return pairs


def send_plane(value, k, x_core):
    return lax.ppermute(value, ("y", "x", "c"), plane_perm(k, x_core))


def pick(value, index):
    return lax.dynamic_index_in_dim(value, index, 0, keepdims=False)


def xor_rows(value, index):
    return jnp.stack([pick(value, index ^ k) for k in range(4)])


def on_device(tokens, gate_up, cotangent):
    rows, feats = tokens.shape
    half = gate_up.shape[2]
    y, zh, x, zl, c = (lax.axis_index(a) for a in AXES)
    shift = y ^ zl
    same = zh == c
    core0 = c == 0
    fwd_a, fwd_b = [(0, 2), (3, 1), (1, 0), (2, 3)], [(1, 2), (2, 1)]
    back_a = [(b, a) for a, b in fwd_a]

    recv_a = lax.ppermute(tokens, ("zh", "c"), fwd_a)
    recv_b = lax.ppermute(tokens, ("zh", "c"), fwd_b)
    own = jnp.where(same, tokens, recv_a)
    sib = jnp.where(same, recv_a, recv_b)
    block = jnp.concatenate([own, sib], axis=1)

    w_own = gate_up.reshape(feats, 2 * half)
    w_sib = lax.ppermute(w_own, "c", xor_perm(2, 1))
    weights = jnp.concatenate([w_own, w_sib], axis=0)

    line = jnp.stack([block] + [send_plane(block, k, 0) for k in (1, 2, 3)])
    size = rows // CHUNKS
    cot = xor_rows(cotangent.reshape(4, rows, half), x)

    hiddens, in_grads, toks, gs = [], [], [], []
    for j in range(CHUNKS):
        part = lax.slice_in_dim(line, j * size, (j + 1) * size, axis=1)
        near, far = send_plane(part, 1, 1), send_plane(part, 3, 1)
        relay = [send_plane(near[:2], 3, 1), send_plane(far[2:], 1, 1)]

        def rows_of(blocks):
            return jnp.concatenate(blocks).reshape(-1, 2 * feats)

        first, last = rows_of([part, near, far]), rows_of(relay)
        flat = jnp.concatenate([first, last])
        pre = jnp.concatenate(
            [jnp.dot(v, weights, preferred_element_type=F32) for v in (first, last)]
        )
        pre = pre.reshape(4, 4, size, 2 * half)

        def slab(k):
            place = shift ^ k
            major = lax.dynamic_index_in_dim(pre, place ^ (place >> 1), 0, keepdims=False)
            minor = lax.dynamic_index_in_dim(pre, place, 1, keepdims=False)
            minor = jnp.concatenate([minor[:2], minor[3:], minor[2:3]])
            return jnp.where(core0, major, minor)

        total = slab(0)
        for k in (1, 2, 3):
            total = total + lax.ppermute(
                slab(k).astype(BF16), "zl", xor_perm(4, k)
            ).astype(F32)
        gate_pre, up_pre = total[..., :half], total[..., half:]
        sigmoid = jax.nn.sigmoid(gate_pre)
        activated = gate_pre * sigmoid
        hiddens.append((activated * up_pre).astype(BF16))
        grad_out = lax.slice_in_dim(cot, j * size, (j + 1) * size, axis=1).astype(F32)
        grad_gate = grad_out * up_pre * sigmoid * (1.0 + gate_pre * (1.0 - sigmoid))
        grad_up = grad_out * activated
        grads = jnp.concatenate([grad_gate, grad_up], axis=-1).astype(BF16)

        gathered = jnp.stack(
            [grads] + [lax.ppermute(grads, "zl", xor_perm(4, k)) for k in (1, 2, 3)]
        )
        ordered = xor_rows(gathered, shift)
        ordered = jnp.where(core0, ordered, jnp.swapaxes(ordered, 0, 1))
        ordered = jnp.concatenate([ordered[:2], ordered[3:], ordered[2:3]])
        g_flat = ordered.reshape(16 * size, 2 * half)
        def back(v):
            out = lax.dot_general(
                v, weights, (((1,), (1,)), ((), ())), preferred_element_type=F32
            )
            return out.reshape(-1, 4, size, 2 * feats)

        cut = 12 * size
        (relay,) = back(g_flat[cut:])
        relay = relay.astype(BF16)
        low, high = send_plane(relay[:2], 1, 1), send_plane(relay[2:], 3, 1)
        out, near, far = back(g_flat[:cut])
        far = jnp.concatenate([far[:2] + low.astype(F32), far[2:]]).astype(BF16)
        near = jnp.concatenate([near[:2], near[2:] + high.astype(F32)]).astype(BF16)
        recv = [send_plane(near, 1, 1), send_plane(far, 3, 1)]
        t_sib = lax.ppermute(flat[:, feats:], "c", xor_perm(2, 1))
        g_sib = lax.ppermute(g_flat, "c", xor_perm(2, 1))
        weight_grad = lax.dot_general(
            jnp.concatenate([flat[:, :feats], t_sib]),
            jnp.concatenate([g_flat, g_sib]),
            (((0,), (0,)), ((), ())),
            preferred_element_type=F32,
        )
        weight_grad = weight_grad.astype(BF16).reshape(feats, 2, half)
        *recv, weight_grad = lax.optimization_barrier((*recv, weight_grad))
        out = out + recv[0].astype(F32) + recv[1].astype(F32)
        part = out[0]
        for k in (1, 2, 3):
            part = part + send_plane(out[k].astype(BF16), k, 0).astype(F32)
        out = part
        g_own, g_sib = out[:, :feats].astype(BF16), out[:, feats:].astype(BF16)
        recv_a = lax.ppermute(jnp.where(same, g_sib, g_own), ("zh", "c"), back_a)
        recv_b = lax.ppermute(g_sib, ("zh", "c"), fwd_b)
        first = jnp.where(same, out[:, :feats], recv_b.astype(F32))
        in_grads.append((first + recv_a.astype(F32)).astype(BF16))
        toks.append(flat)
        gs.append(g_flat)

    hidden = xor_rows(jnp.concatenate(hiddens, axis=1), x).reshape(4 * rows, half)
    return hidden, jnp.concatenate(in_grads, axis=0), weight_grad


def solution(mesh):
    split = Mesh(mesh.devices.reshape(4, 2, 4, 4, 2), AXES)
    row, col = ("y", "zh", "x"), ("zl", "c")
    in_specs = (P(row, col), P(col, None, row), P(col, row))
    out_specs = (P(col, row), P(row, col), P(col, None, row))
    return jax.shard_map(
        on_device, mesh=split, in_specs=in_specs, out_specs=out_specs, check_vma=False
    )
```

```python
import jax
import jax.numpy as jnp
from jax import lax
from jax.experimental.layout import Layout, with_layout_constraint
from jax.sharding import Mesh
from jax.sharding import PartitionSpec as P

AXES = ("y", "zh", "x", "zl", "c")
ORDER = (0, 1, 3, 2)
BF16 = jnp.bfloat16
F32 = jnp.float32


def xor_perm(n, k):
    return [(i, i ^ k) for i in range(n)]


def plane_perm(k, x_core):
    pairs = []
    for y in range(4):
        for x in range(4):
            for c in range(2):
                y2, x2 = (y, x ^ k) if c == x_core else (y ^ k, x)
                pairs.append(((y * 4 + x) * 2 + c, (y2 * 4 + x2) * 2 + c))
    return pairs


def send_plane(value, k, x_core):
    return lax.ppermute(value, ("y", "x", "c"), plane_perm(k, x_core))


def pick(value, index):
    return lax.dynamic_index_in_dim(value, index, 0, keepdims=False)


def xor_rows(value, index):
    return jnp.stack([pick(value, index ^ k) for k in ORDER])


def on_device(tokens, gate_up, cotangent):
    rows, feats = tokens.shape
    half = gate_up.shape[2]
    y, zh, x, zl, c = (lax.axis_index(a) for a in AXES)
    shift = y ^ zl
    same = zh == c
    core0 = c == 0
    fwd_a, fwd_b = [(0, 2), (3, 1), (1, 0), (2, 3)], [(1, 2), (2, 1)]
    back_a = [(b, a) for a, b in fwd_a]

    recv_a = lax.ppermute(tokens, ("zh", "c"), fwd_a)
    recv_b = lax.ppermute(tokens, ("zh", "c"), fwd_b)
    own = jnp.where(same, tokens, recv_a)
    sib = jnp.where(same, recv_a, recv_b)
    block = jnp.concatenate([own, sib], axis=1)

    w_own = gate_up.reshape(feats, 2 * half)
    w_sib = lax.ppermute(w_own, "c", xor_perm(2, 1))
    weights = jnp.concatenate([w_own, w_sib], axis=0)

    part = jnp.stack([block] + [send_plane(block, k, 0) for k in ORDER[1:]])
    size = rows
    cot = xor_rows(cotangent.reshape(4, rows, half), x)

    near, far = send_plane(part, 1, 1), send_plane(part, 3, 1)
    relay = [send_plane(near[:2], 3, 1), send_plane(far[2:], 1, 1)]

    def rows_of(blocks):
        return jnp.concatenate(blocks).reshape(-1, 2 * feats)

    first = lax.optimization_barrier(rows_of([part, near, far]))
    head = jnp.dot(first, weights, preferred_element_type=F32)
    head, *relay = lax.optimization_barrier((head, *relay))
    last = rows_of(relay)
    pre = jnp.concatenate([head, jnp.dot(last, weights, preferred_element_type=F32)])
    pre = pre.reshape(4, 4, size, 2 * half)

    def slab(k):
        place = shift ^ k
        place = place ^ (place >> 1)
        major = lax.dynamic_index_in_dim(pre, place, 0, keepdims=False)
        minor = lax.dynamic_index_in_dim(pre, place, 1, keepdims=False)
        return jnp.where(core0, major, minor)

    total = slab(0)
    for k in (1, 2, 3):
        total = total + lax.ppermute(
            slab(k).astype(BF16), "zl", xor_perm(4, k)
        ).astype(F32)
    gate_pre, up_pre = total[..., :half], total[..., half:]
    sigmoid = jax.nn.sigmoid(gate_pre)
    activated = gate_pre * sigmoid
    hidden = (activated * up_pre).astype(BF16)
    grad_out = cot.astype(F32)
    grad_gate = grad_out * up_pre * sigmoid * (1.0 + gate_pre * (1.0 - sigmoid))
    grad_up = grad_out * activated
    grads = jnp.concatenate([grad_gate, grad_up], axis=-1).astype(BF16)

    gathered = jnp.stack(
        [grads] + [lax.ppermute(grads, "zl", xor_perm(4, k)) for k in (1, 2, 3)]
    )
    ordered = xor_rows(gathered, shift)
    ordered = jnp.where(core0, ordered, jnp.swapaxes(ordered, 0, 1))
    g_flat = ordered.reshape(16 * size, 2 * half)

    def back(v):
        out = lax.dot_general(
            v, weights, (((1,), (1,)), ((), ())), preferred_element_type=F32
        )
        return out.reshape(-1, 4, size, 2 * feats)

    cut = 12 * size
    (relay,) = back(g_flat[cut:])
    relay = relay.astype(BF16)
    low, high = send_plane(relay[:2], 1, 1), send_plane(relay[2:], 3, 1)
    out, near, far = back(g_flat[:cut])
    far = jnp.concatenate([far[:2] + low.astype(F32), far[2:]]).astype(BF16)
    near = jnp.concatenate([near[:2], near[2:] + high.astype(F32)]).astype(BF16)
    recv = [send_plane(near, 1, 1), send_plane(far, 3, 1)]
    t_sib = jnp.concatenate([first[:, feats:], last[:, feats:]])
    t_sib = lax.ppermute(t_sib, "c", xor_perm(2, 1))
    g_sib = lax.ppermute(g_flat, "c", xor_perm(2, 1))
    weight_grad = lax.dot_general(
        jnp.concatenate([first[:, :feats], last[:, :feats], t_sib]),
        jnp.concatenate([g_flat, g_sib]),
        (((0,), (0,)), ((), ())),
        preferred_element_type=F32,
    )
    weight_grad = weight_grad.astype(BF16)
    *recv, weight_grad = lax.optimization_barrier((*recv, weight_grad))
    out = out + recv[0].astype(F32) + recv[1].astype(F32)
    part = out[0]
    recv = [send_plane(out[i].astype(BF16), ORDER[i], 0) for i in (1, 2, 3)]
    weight_grad = weight_grad.reshape(feats, 2, half)
    weight_grad = with_layout_constraint(weight_grad, Layout((0, 1, 2)))
    *recv, weight_grad = lax.optimization_barrier((*recv, weight_grad))
    for v in recv:
        part = part + v.astype(F32)
    out = part
    g_own, g_sib = out[:, :feats].astype(BF16), out[:, feats:].astype(BF16)
    recv_a = lax.ppermute(jnp.where(same, g_sib, g_own), ("zh", "c"), back_a)
    recv_b = lax.ppermute(g_sib, ("zh", "c"), fwd_b)
    first = jnp.where(same, out[:, :feats], recv_b.astype(F32))
    input_grad = (first + recv_a.astype(F32)).astype(BF16)

    places = [(x ^ k) ^ ((x ^ k) >> 1) for k in range(4)]
    hidden = jnp.stack([pick(hidden, p) for p in places]).reshape(4 * rows, half)
    return hidden, input_grad, weight_grad


def solution(mesh):
    split = Mesh(mesh.devices.reshape(4, 2, 4, 4, 2), AXES)
    row, col = ("y", "zh", "x"), ("zl", "c")
    in_specs = (P(row, col), P(col, None, row), P(col, row))
    out_specs = (P(col, row), P(row, col), P(col, None, row))
    return jax.shard_map(
        on_device, mesh=split, in_specs=in_specs, out_specs=out_specs, check_vma=False
    )
```

```python
import jax
import jax.numpy as jnp
from jax import lax
from jax.experimental.layout import Layout, with_layout_constraint
from jax.sharding import Mesh
from jax.sharding import PartitionSpec as P

AXES = ("y", "zh", "x", "zl", "c")
ORDER = (0, 1, 3, 2)
BF16 = jnp.bfloat16
F32 = jnp.float32


def xor_perm(n, k):
    return [(i, i ^ k) for i in range(n)]


def plane_perm(k, x_core):
    pairs = []
    for y in range(4):
        for x in range(4):
            for c in range(2):
                y2, x2 = (y, x ^ k) if c == x_core else (y ^ k, x)
                pairs.append(((y * 4 + x) * 2 + c, (y2 * 4 + x2) * 2 + c))
    return pairs


def send_plane(value, k, x_core):
    return lax.ppermute(value, ("y", "x", "c"), plane_perm(k, x_core))


def pick(value, index):
    return lax.dynamic_index_in_dim(value, index, 0, keepdims=False)


def xor_rows(value, index):
    return jnp.stack([pick(value, index ^ k) for k in ORDER])


def on_device(tokens, gate_up, cotangent):
    rows, feats = tokens.shape
    half = gate_up.shape[2]
    y, zh, x, zl, c = (lax.axis_index(a) for a in AXES)
    shift = y ^ zl
    same = zh == c
    core0 = c == 0
    fwd_a, fwd_b = [(0, 2), (3, 1), (1, 0), (2, 3)], [(1, 2), (2, 1)]
    back_a = [(b, a) for a, b in fwd_a]

    recv_a = lax.ppermute(tokens, ("zh", "c"), fwd_a)
    recv_b = lax.ppermute(tokens, ("zh", "c"), fwd_b)
    own = jnp.where(same, tokens, recv_a)
    sib = jnp.where(same, recv_a, recv_b)
    block = jnp.concatenate([own, sib], axis=1)

    w_own = gate_up.reshape(feats, 2 * half)
    w_sib = lax.ppermute(w_own, "c", xor_perm(2, 1))
    weights = jnp.concatenate([w_own, w_sib], axis=0)

    part = jnp.stack([block] + [send_plane(block, k, 0) for k in ORDER[1:]])
    size = rows
    cot = xor_rows(cotangent.reshape(4, rows, half), x)

    near, far = send_plane(part, 1, 1), send_plane(part, 3, 1)
    relay = [send_plane(near[:2], 3, 1), send_plane(far[2:], 1, 1)]

    def rows_of(blocks):
        return jnp.concatenate(blocks).reshape(-1, 2 * feats)

    first = lax.optimization_barrier(rows_of([part, near, far]))
    head = jnp.dot(first, weights, preferred_element_type=F32)
    head, *relay = lax.optimization_barrier((head, *relay))
    last = rows_of(relay)
    pre = jnp.concatenate([head, jnp.dot(last, weights, preferred_element_type=F32)])
    pre = pre.reshape(4, 4, size, 2 * half)

    def slab(k):
        place = shift ^ k
        place = place ^ (place >> 1)
        major = lax.dynamic_index_in_dim(pre, place, 0, keepdims=False)
        minor = lax.dynamic_index_in_dim(pre, place, 1, keepdims=False)
        return jnp.where(core0, major, minor)

    total, *sends = lax.optimization_barrier(
        (slab(0), *(slab(k).astype(BF16) for k in (1, 2, 3)))
    )
    for k, send in zip((1, 2, 3), sends):
        total = total + lax.ppermute(send, "zl", xor_perm(4, k)).astype(F32)
    gate_pre, up_pre = total[..., :half], total[..., half:]
    sigmoid = jax.nn.sigmoid(gate_pre)
    activated = gate_pre * sigmoid
    hidden = (activated * up_pre).astype(BF16)
    grad_out = cot.astype(F32)
    grad_gate = grad_out * up_pre * sigmoid * (1.0 + gate_pre * (1.0 - sigmoid))
    grad_up = grad_out * activated
    grads = jnp.concatenate([grad_gate, grad_up], axis=-1).astype(BF16)

    gathered = jnp.stack(
        [grads] + [lax.ppermute(grads, "zl", xor_perm(4, k)) for k in (1, 2, 3)]
    )
    ordered = xor_rows(gathered, shift)
    ordered = jnp.where(core0, ordered, jnp.swapaxes(ordered, 0, 1))
    g_flat = ordered.reshape(16 * size, 2 * half)

    def back(v):
        out = lax.dot_general(
            v, weights, (((1,), (1,)), ((), ())), preferred_element_type=F32
        )
        return out.reshape(-1, 4, size, 2 * feats)

    cut = 12 * size
    (relay,) = back(g_flat[cut:])
    relay = relay.astype(BF16)
    low, high = send_plane(relay[:2], 1, 1), send_plane(relay[2:], 3, 1)
    out, near, far = back(g_flat[:cut])
    far = jnp.concatenate([far[:2] + low.astype(F32), far[2:]]).astype(BF16)
    near = jnp.concatenate([near[:2], near[2:] + high.astype(F32)]).astype(BF16)
    recv = [send_plane(near, 1, 1), send_plane(far, 3, 1)]
    t_sib = jnp.concatenate([first[:, feats:], last[:, feats:]])
    t_sib = lax.ppermute(t_sib, "c", xor_perm(2, 1))
    g_sib = lax.ppermute(g_flat, "c", xor_perm(2, 1))
    weight_grad = lax.dot_general(
        jnp.concatenate([first[:, :feats], last[:, :feats], t_sib]),
        jnp.concatenate([g_flat, g_sib]),
        (((0,), (0,)), ((), ())),
        preferred_element_type=F32,
    )
    weight_grad = weight_grad.astype(BF16)
    *recv, weight_grad = lax.optimization_barrier((*recv, weight_grad))
    out = out + recv[0].astype(F32) + recv[1].astype(F32)
    part = out[0]
    recv = [send_plane(out[i].astype(BF16), ORDER[i], 0) for i in (1, 2, 3)]
    weight_grad = weight_grad.reshape(feats, 2, half)
    weight_grad = with_layout_constraint(weight_grad, Layout((0, 1, 2)))
    *recv, weight_grad = lax.optimization_barrier((*recv, weight_grad))
    for v in recv:
        part = part + v.astype(F32)
    out = part
    g_own, g_sib = out[:, :feats].astype(BF16), out[:, feats:].astype(BF16)
    recv_a = lax.ppermute(jnp.where(same, g_sib, g_own), ("zh", "c"), back_a)
    recv_b = lax.ppermute(g_sib, ("zh", "c"), fwd_b)
    first = jnp.where(same, out[:, :feats], recv_b.astype(F32))
    input_grad = (first + recv_a.astype(F32)).astype(BF16)

    places = [(x ^ k) ^ ((x ^ k) >> 1) for k in range(4)]
    hidden = jnp.stack([pick(hidden, p) for p in places]).reshape(4 * rows, half)
    return hidden, input_grad, weight_grad


def solution(mesh):
    split = Mesh(mesh.devices.reshape(4, 2, 4, 4, 2), AXES)
    row, col = ("y", "zh", "x"), ("zl", "c")
    in_specs = (P(row, col), P(col, None, row), P(col, row))
    out_specs = (P(col, row), P(row, col), P(col, None, row))
    return jax.shard_map(
        on_device, mesh=split, in_specs=in_specs, out_specs=out_specs, check_vma=False
    )
```

```python
import jax
import jax.numpy as jnp
from jax import lax
from jax.experimental.layout import Layout, with_layout_constraint
from jax.sharding import Mesh
from jax.sharding import PartitionSpec as P

AXES = ("y", "zh", "x", "zl", "c")
ORDER = (0, 1, 3, 2)
BF16 = jnp.bfloat16
F32 = jnp.float32


def xor_perm(n, k):
    return [(i, i ^ k) for i in range(n)]


def plane_perm(k, x_core):
    pairs = []
    for y in range(4):
        for x in range(4):
            for c in range(2):
                y2, x2 = (y, x ^ k) if c == x_core else (y ^ k, x)
                pairs.append(((y * 4 + x) * 2 + c, (y2 * 4 + x2) * 2 + c))
    return pairs


def send_plane(value, k, x_core):
    return lax.ppermute(value, ("y", "x", "c"), plane_perm(k, x_core))


def pick(value, index):
    return lax.dynamic_index_in_dim(value, index, 0, keepdims=False)


def xor_rows(value, index):
    return jnp.stack([pick(value, index ^ k) for k in ORDER])


def on_device(tokens, gate_up, cotangent):
    rows, feats = tokens.shape
    half = gate_up.shape[2]
    y, zh, x, zl, c = (lax.axis_index(a) for a in AXES)
    shift = y ^ zl
    same = zh == c
    core0 = c == 0
    fwd_a, fwd_b = [(0, 2), (3, 1), (1, 0), (2, 3)], [(1, 2), (2, 1)]
    back_a = [(b, a) for a, b in fwd_a]

    recv_a = lax.ppermute(tokens, ("zh", "c"), fwd_a)
    recv_b = lax.ppermute(tokens, ("zh", "c"), fwd_b)
    own = jnp.where(same, tokens, recv_a)
    sib = jnp.where(same, recv_a, recv_b)
    block = jnp.concatenate([own, sib], axis=1)

    w_own = gate_up.reshape(feats, 2 * half)
    w_sib = lax.ppermute(w_own, "c", xor_perm(2, 1))
    weights = jnp.concatenate([w_own, w_sib], axis=0)

    part = jnp.stack([block] + [send_plane(block, k, 0) for k in ORDER[1:]])
    size = rows
    cot = xor_rows(cotangent.reshape(4, rows, half), x)

    near, far = send_plane(part, 1, 1), send_plane(part, 3, 1)
    relay = [send_plane(near[:2], 3, 1), send_plane(far[2:], 1, 1)]

    def rows_of(blocks):
        return jnp.concatenate(blocks).reshape(-1, 2 * feats)

    first = lax.optimization_barrier(rows_of([part, near, far]))
    head = jnp.dot(first, weights, preferred_element_type=F32)
    head, *relay = lax.optimization_barrier((head, *relay))
    last = rows_of(relay)
    pre = jnp.concatenate([head, jnp.dot(last, weights, preferred_element_type=F32)])
    pre = pre.reshape(4, 4, size, 2 * half)

    def slab(k):
        place = shift ^ k
        place = place ^ (place >> 1)
        major = lax.dynamic_index_in_dim(pre, place, 0, keepdims=False)
        minor = lax.dynamic_index_in_dim(pre, place, 1, keepdims=False)
        return jnp.where(core0, major, minor)

    total, *sends = lax.optimization_barrier(
        (slab(0), *(slab(k).astype(BF16) for k in (3, 2, 1)))
    )
    for k, send in zip((3, 2, 1), sends):
        total = total + lax.ppermute(send, "zl", xor_perm(4, k)).astype(F32)
    gate_pre, up_pre = total[..., :half], total[..., half:]
    sigmoid = jax.nn.sigmoid(gate_pre)
    activated = gate_pre * sigmoid
    hidden = (activated * up_pre).astype(BF16)
    grad_out = cot.astype(F32)
    grad_gate = grad_out * up_pre * sigmoid * (1.0 + gate_pre * (1.0 - sigmoid))
    grad_up = grad_out * activated
    grads = jnp.concatenate([grad_gate, grad_up], axis=-1).astype(BF16)

    gathered = jnp.stack(
        [grads] + [lax.ppermute(grads, "zl", xor_perm(4, k)) for k in (1, 2, 3)]
    )
    ordered = xor_rows(gathered, shift)
    ordered = jnp.where(core0, ordered, jnp.swapaxes(ordered, 0, 1))
    g_flat = ordered.reshape(16 * size, 2 * half)

    def back(v):
        out = lax.dot_general(
            v, weights, (((1,), (1,)), ((), ())), preferred_element_type=F32
        )
        return out.reshape(-1, 4, size, 2 * feats)

    cut = 12 * size
    (relay,) = back(g_flat[cut:])
    relay = relay.astype(BF16)
    low, high = send_plane(relay[:2], 1, 1), send_plane(relay[2:], 3, 1)
    out, near, far = back(g_flat[:cut])
    far = jnp.concatenate([far[:2] + low.astype(F32), far[2:]]).astype(BF16)
    near = jnp.concatenate([near[:2], near[2:] + high.astype(F32)]).astype(BF16)
    recv = [send_plane(near, 1, 1), send_plane(far, 3, 1)]
    t_sib = jnp.concatenate([first[:, feats:], last[:, feats:]])
    t_sib = lax.ppermute(t_sib, "c", xor_perm(2, 1))
    g_sib = lax.ppermute(g_flat, "c", xor_perm(2, 1))
    weight_grad = lax.dot_general(
        jnp.concatenate([first[:, :feats], last[:, :feats], t_sib]),
        jnp.concatenate([g_flat, g_sib]),
        (((0,), (0,)), ((), ())),
        preferred_element_type=F32,
    )
    weight_grad = weight_grad.astype(BF16)
    *recv, weight_grad = lax.optimization_barrier((*recv, weight_grad))
    out = out + recv[0].astype(F32) + recv[1].astype(F32)
    part = out[0]
    recv = [send_plane(out[i].astype(BF16), ORDER[i], 0) for i in (1, 2, 3)]
    weight_grad = weight_grad.reshape(feats, 2, half)
    weight_grad = with_layout_constraint(weight_grad, Layout((0, 1, 2)))
    *recv, weight_grad = lax.optimization_barrier((*recv, weight_grad))
    for v in recv:
        part = part + v.astype(F32)
    out = part
    g_own, g_sib = out[:, :feats].astype(BF16), out[:, feats:].astype(BF16)
    recv_a = lax.ppermute(jnp.where(same, g_sib, g_own), ("zh", "c"), back_a)
    recv_b = lax.ppermute(g_sib, ("zh", "c"), fwd_b)
    first = jnp.where(same, out[:, :feats], recv_b.astype(F32))
    input_grad = (first + recv_a.astype(F32)).astype(BF16)

    places = [(x ^ k) ^ ((x ^ k) >> 1) for k in range(4)]
    hidden = jnp.stack([pick(hidden, p) for p in places]).reshape(4 * rows, half)
    return hidden, input_grad, weight_grad


def solution(mesh):
    split = Mesh(mesh.devices.reshape(4, 2, 4, 4, 2), AXES)
    row, col = ("y", "zh", "x"), ("zl", "c")
    in_specs = (P(row, col), P(col, None, row), P(col, row))
    out_specs = (P(col, row), P(row, col), P(col, None, row))
    return jax.shard_map(
        on_device, mesh=split, in_specs=in_specs, out_specs=out_specs, check_vma=False
    )
```
